32 devices in a mesh: bond: 16 (over z, y, x), op: 2 (over core).
Axes of the slice: x: 2, y: 2, z: 4, core: 2. Of those that a mesh axis runs over, the one named last changes fastest.
Arguments:
- wavefunction: float32 [6, 256, 8192], P(None, None, 'bond'), may hold values from -6 to 6
- left_tiles: bfloat16 [16, 16, 2, 128, 128], P('op', None, None, 'bond'), may hold values from -0.375 to 0.375
- right_tiles: bfloat16 [16, 16, 2, 128, 128], P('op', None, None, 'bond'), may hold values from -0.375 to 0.375
- site_operators: float32 [16, 4, 4], P('op'), may hold values from -1.75 to 1.75
- left_charge: int32 [16], replicated, may hold values from 0 to 7, as said below
- right_charge: int32 [16], replicated, may hold values from 0 to 7, as said below
- channel_charge: int32 [16, 2], replicated, may hold values from -1 to 7, as said below
Outputs:
- sigma_one: float32 [6, 256, 8192], P(None, 'bond', 'op')
- sigma_two: float32 [6, 256, 8192], P(None, 'op', 'bond')
The draws below stay inside these ranges and needn't reach their ends.
Inputs may be any that keep to these rules, and one draw needn't show every extreme that they name: `left_charge`: each charge labels exactly 2 of the left blocks. `right_charge`: each charge labels exactly 2 of the right blocks. `channel_charge`: column 0 is a left charge shift, each of 0 to 7 used by exactly 2 channels; column 1 is a site charge shift, each of -1, 0 and 1 used by 5 or 6 channels.
All inputs are finite; a program needn't handle non-finite values.
Results may differ from the reference program's by a relative error of at most 0.0057.
Values may be sent and summed in bfloat16 or wider, within the bound.
A program may use at most 128 MiB of HBM per device.

```python
import jax
import jax.numpy as jnp
from jax import lax

M = 2048
B = 128
NQ = 8
DP = 4
C = 16
K = 6
NB = 16
NPB = 2
NS = 256


def draw_left_charge(key, part):
    ordering = jax.random.permutation(jax.random.fold_in(key, 11), NB)
    return (ordering % NQ).astype(jnp.int32)


def draw_right_charge(key, part):
    ordering = jax.random.permutation(jax.random.fold_in(key, 23), NB)
    return (ordering % NQ).astype(jnp.int32)


def draw_channel_charge(key, part):
    shifts = jax.random.permutation(jax.random.fold_in(key, 31), C) % NQ
    moves = jax.random.permutation(jax.random.fold_in(key, 37), C) % 3 - 1
    return jnp.stack([shifts, moves], axis=1).astype(jnp.int32)


def levels(key, dims, shards, least, top_value):
    def one(axis_at, shards_of):
        heights = jax.random.uniform(jax.random.fold_in(jax.random.fold_in(key, 6), axis_at), (shards_of,), jnp.float32, least / len(shards), top_value / len(shards))
        return jnp.repeat(jnp.exp(heights), dims[axis_at] // shards_of).reshape((-1,) + (1,) * (len(dims) - axis_at - 1))

    level = one(*shards[0])
    for cut in shards[1:]:
        level = level * one(*cut)
    return level


def centred(own_key, dims, deviation, limit, shards=(), held_as=jnp.bfloat16):
    entries = deviation * jax.random.normal(own_key, dims, jnp.float32)
    if shards:
        entries = entries * levels(own_key, dims, shards, -0.22, 0.18)
    return jnp.clip(entries, -limit, limit).astype(held_as)


def setup_inputs(seed: int = 0) -> dict:
    seeds = jax.random.split(jax.random.key(seed), 8)
    return {
        "wavefunction": centred(seeds[0], (K, NS, DP * M), 1.0, 6.0, ((2, 16),), jnp.float32),
        "left_tiles": centred(seeds[1], (C, NB, NPB, B, B), (NPB * B) ** -0.5, 0.375, ((0, 2), (3, 16))),
        "right_tiles": centred(seeds[2], (C, NB, NPB, B, B), (NPB * B) ** -0.5, 0.375, ((0, 2), (3, 16))),
        "site_operators": centred(seeds[3], (C, DP, DP), (3 * DP) ** -0.5, 1.75, ((0, 2),), jnp.float32),
        "left_charge": draw_left_charge(jax.random.fold_in(seeds[7], 71), 0),
        "right_charge": draw_right_charge(jax.random.fold_in(seeds[7], 71), 0),
        "channel_charge": draw_channel_charge(jax.random.fold_in(seeds[7], 71), 0),
    }


site_charge_table = (0, 1, 1, 2)


def block_sources(charge, offset):
    ordering = jnp.argsort(charge, stable=True).astype(jnp.int32)
    target = (charge - offset) % NQ
    slot_index = target[:, None] * NPB + jnp.arange(NPB, dtype=jnp.int32)[None, :]
    return ordering[slot_index]


def site_masks(site_operators, channel_charge):
    site_charge = jnp.array(site_charge_table, dtype=jnp.int32)
    charge_step = site_charge[:, None] - site_charge[None, :]
    allowed = (charge_step[None, :, :] - channel_charge[:, 1][:, None, None]) % NQ == 0
    return jnp.where(allowed, site_operators, jnp.zeros_like(site_operators))


def column_classes(right_charge):
    site_charge = jnp.array(site_charge_table, dtype=jnp.int32)
    starts = jnp.arange(DP * NB, dtype=jnp.int32) * B
    return (site_charge[starts // M] + right_charge[(starts % M) // B]) % NQ


def left_pass(left_set, left_order, row_class, values):
    group_count = row_class.shape[0]
    slots = row_class[:, None] * NPB + jnp.arange(NPB, dtype=jnp.int32)[None, :]
    picked_tiles = left_set[left_order[slots]].astype(jnp.float32)
    blocks = values.reshape(values.shape[0], NPB, B, group_count, B).astype(jnp.float32)
    result = jnp.einsum('gmnab,knbgw->kmagw', picked_tiles, blocks, precision=lax.Precision.HIGHEST)
    return result.reshape(values.shape)


def right_pass(right_set, sources, site_matrix, values):
    root_count = values.shape[0]
    row_count = values.shape[1]
    blocks = values.reshape(root_count, row_count, DP, NB, B)
    picked = blocks[:, :, :, sources].astype(jnp.float32)
    inner_sum = jnp.einsum('jnab,kspjnb->kspja', right_set.astype(jnp.float32), picked,
                           precision=lax.Precision.HIGHEST)
    mixture = jnp.einsum('pq,ksqja->kspja', site_matrix, inner_sum, precision=lax.Precision.HIGHEST)
    return mixture.reshape(values.shape)


def reference(wavefunction, left_tiles, right_tiles, site_operators, left_charge, right_charge, channel_charge):
    sector_psi = lax.optimization_barrier(wavefunction.astype(jnp.bfloat16))
    left_order = jnp.argsort(left_charge, stable=True).astype(jnp.int32)
    classes = column_classes(right_charge)
    right_offsets = -(channel_charge[:, 0] + channel_charge[:, 1])
    right_sources = jax.vmap(block_sources, in_axes=(None, 0))(right_charge, right_offsets)
    site_matrices = site_masks(site_operators, channel_charge)
    channel_items = (left_tiles, right_tiles, right_sources, site_matrices, channel_charge[:, 0])

    def first_pass(running, items):
        left_set, right_set, right_src, site_matrix, shift = items
        row_class = (shift - classes) % NQ
        left_side = lax.optimization_barrier(
            left_pass(left_set, left_order, row_class, sector_psi).astype(jnp.bfloat16))
        return running + right_pass(right_set, right_src, site_matrix, left_side), None

    sigma_one, unused_one = lax.scan(first_pass, jnp.zeros(wavefunction.shape, jnp.float32), channel_items)
    rounded_one = lax.optimization_barrier(sigma_one.astype(jnp.bfloat16))
    second_class = (-classes) % NQ

    def second_pass(running, items):
        left_set, right_set, right_src, site_matrix, shift = items
        right_side = lax.optimization_barrier(
            right_pass(right_set, right_src, site_matrix, rounded_one).astype(jnp.bfloat16))
        return running + left_pass(left_set, left_order, second_class, right_side), None

    sigma_two, unused_two = lax.scan(second_pass, jnp.zeros(wavefunction.shape, jnp.float32), channel_items)
    return sigma_one, sigma_two
```

```python
import functools

import jax
import jax.numpy as jnp
from jax import lax
from jax.experimental import pallas as pl
from jax.experimental.pallas import tpu as pltpu
from jax.sharding import PartitionSpec as P

M = 2048
B = 128
NQ = 8
DP = 4
NB = 16
NPB = 2

site_charge_table = (0, 1, 1, 2)
MESH = pl.DeviceIdType.MESH


def site_masks(site_operators, channel_charge):
    site_charge = jnp.array(site_charge_table, dtype=jnp.int32)
    charge_step = site_charge[:, None] - site_charge[None, :]
    allowed = (charge_step[None, :, :] - channel_charge[:, 1][:, None, None]) % NQ == 0
    return jnp.where(allowed, site_operators, jnp.zeros_like(site_operators))


def spread_kernel(half, ops, x_ref, g_ref, own_sem, send_sem, recv_sem, fsend, frecv):
    bond = lax.axis_index("bond")
    o = lax.axis_index("op")
    i = lax.rem(bond, half)
    base = bond - i

    barrier = pltpu.get_barrier_semaphore()
    for d in range(1, half):
        pl.semaphore_signal(
            barrier, inc=1, device_id={"bond": base + lax.rem(i + d, half), "op": o},
            device_id_type=MESH,
        )
    for e in range(1, ops):
        pl.semaphore_signal(
            barrier, inc=1, device_id={"bond": bond, "op": lax.rem(o + e, ops)},
            device_id_type=MESH,
        )
    pl.semaphore_wait(barrier, half - 1 + ops - 1)

    copies = []
    for d in range(1, half):
        copy = pltpu.make_async_remote_copy(
            src_ref=x_ref, dst_ref=g_ref.at[i, o], send_sem=send_sem.at[d], recv_sem=recv_sem.at[d],
            device_id={"bond": base + lax.rem(i + d, half), "op": o}, device_id_type=MESH,
        )
        copy.start()
        copies.append(copy)

    def forward(d, src, slot):
        sent = []
        for e in range(1, ops):
            copy = pltpu.make_async_remote_copy(
                src_ref=src, dst_ref=g_ref.at[slot, o],
                send_sem=fsend.at[d, e], recv_sem=frecv.at[d, e],
                device_id={"bond": bond, "op": lax.rem(o + e, ops)}, device_id_type=MESH,
            )
            copy.start()
            sent.append(copy)
        return sent

    forwards = forward(0, x_ref, i)
    own = pltpu.make_async_copy(x_ref, g_ref.at[i, o], own_sem)
    own.start()
    for d in range(1, half):
        copies[d - 1].wait_recv()
        slot = lax.rem(i - d + half, half)
        forwards += forward(d, g_ref.at[slot, o], slot)
    own.wait()
    for copy in copies:
        copy.wait_send()
    for copy in forwards:
        copy.wait()


def spread(x, half, ops, collective_id):
    return pl.pallas_call(
        functools.partial(spread_kernel, half, ops),
        out_shape=jax.ShapeDtypeStruct((half, ops) + x.shape, x.dtype),
        in_specs=[pl.BlockSpec(memory_space=pltpu.VMEM)],
        out_specs=pl.BlockSpec(memory_space=pl.ANY),
        scratch_shapes=[
            pltpu.SemaphoreType.DMA,
            pltpu.SemaphoreType.DMA((half,)),
            pltpu.SemaphoreType.DMA((half,)),
            pltpu.SemaphoreType.DMA((half, ops)),
            pltpu.SemaphoreType.DMA((half, ops)),
        ],
        compiler_params=pltpu.CompilerParams(collective_id=collective_id, has_side_effects=True),
        name=f"spread_{collective_id}",
    )(x)


def apply_kernel(
    channels, rows, roots, site_charges,
    order_ref, shift_ref, site_ref, psi_ref, left_ref, right_ref, out_ref, mixed
):
    @pl.loop(0, NQ)
    def _(g):
        for n in range(NPB):
            r = order_ref[g * NPB + n]
            terms = []
            for q in range(DP):
                h = lax.rem(2 * NQ - site_charges[q] - g, NQ)
                terms.append(
                    jnp.dot(left_ref[h], psi_ref[q * NB + r], preferred_element_type=jnp.float32)
                )
            for c in range(channels):
                for p in range(DP):
                    total = site_ref[(c * DP + p) * DP] * terms[0][c * rows:(c + 1) * rows]
                    for q in range(1, DP):
                        total += site_ref[(c * DP + p) * DP + q] * terms[q][c * rows:(c + 1) * rows]
                    total = total.astype(jnp.bfloat16)
                    for k in range(roots):
                        at = (p * roots + k) * rows
                        mixed[c, g, at:at + rows, n * B:(n + 1) * B] = total[:, k * B:(k + 1) * B]

    @pl.loop(0, NQ)
    def _(g):
        total = None
        for c in range(channels):
            source = lax.rem(g + shift_ref[c], NQ)
            term = lax.dot_general(
                mixed[c, source], right_ref[c, g], (((1,), (1,)), ((), ())),
                preferred_element_type=jnp.float32,
            )
            total = term if total is None else total + term
        for m in range(NPB):
            out_ref[order_ref[g * NPB + m]] = total[:, m * B:(m + 1) * B]


def apply_all(order, shift, site, psi, left, right, rows, roots):
    channels = right.shape[0]
    height = DP * roots * rows
    smem = pl.BlockSpec(memory_space=pltpu.SMEM)
    vmem = pl.BlockSpec(memory_space=pltpu.VMEM)
    return pl.pallas_call(
        functools.partial(apply_kernel, channels, rows, roots, site_charge_table),
        out_shape=jax.ShapeDtypeStruct((NB, height, B), jnp.float32),
        in_specs=[smem, smem, smem, vmem, vmem, vmem],
        out_specs=vmem,
        scratch_shapes=[pltpu.VMEM((channels, NQ, height, NPB * B), jnp.bfloat16)],
        compiler_params=pltpu.CompilerParams(vmem_limit_bytes=58 * 1024 * 1024),
        name="apply_all",
    )(order, shift, site, psi, left, right)


def local(
    wavefunction, left_tiles, right_tiles, site_operators, left_charge, right_charge, channel_charge
):
    bonds = lax.axis_size("bond")
    ops = lax.axis_size("op")
    bond = lax.axis_index("bond")
    op = lax.axis_index("op")
    roots, sector_rows, strip = wavefunction.shape
    channels = site_operators.shape[0]
    half = bonds // 2
    part = bond // half
    some = roots // 2
    chunk = left_tiles.shape[3]
    band = 2 * chunk
    rows = NPB * band
    held = -(-rows // 16) * 16
    width = min(strip, B)
    groups = strip // width
    own_charge = lax.dynamic_slice_in_dim(channel_charge, op * channels, channels, 0)
    left_order = jnp.argsort(left_charge, stable=True).astype(jnp.int32)
    right_order = jnp.argsort(right_charge, stable=True).astype(jnp.int32)
    shift = (own_charge[:, 0] + own_charge[:, 1]) % NQ
    site = site_masks(site_operators, own_charge).reshape(-1)
    partner = [(b, (b + half) % bonds) for b in range(bonds)]

    right = right_tiles[:, right_order].transpose(0, 1, 3, 2, 4).reshape(
        channels, NB, chunk, NPB * B
    )
    right = lax.all_gather(right, "bond", axis=2, tiled=True).reshape(
        channels, NQ, NPB * B, NPB * B
    )

    even = [(b, b // 2 + (b % 2) * half) for b in range(bonds)]
    odd = [(b, b // 2 + (1 - b % 2) * half) for b in range(bonds)]
    one = lax.ppermute(left_tiles, "bond", even)
    two = lax.ppermute(left_tiles, "bond", odd)
    low = jnp.where(part == 0, one, two)
    high = jnp.where(part == 0, two, one)
    left = jnp.concatenate([low, high], axis=3)
    left_slots = ((jnp.arange(NQ)[:, None] + own_charge[None, :, 0]) % NQ)[:, :, None] * NPB + jnp.arange(NPB)
    left = left[jnp.arange(channels)[None, :, None], left_order[left_slots]]
    left = left.transpose(0, 1, 2, 4, 3, 5).reshape(NQ, channels, rows, NPB * B)
    left = jnp.pad(left, ((0, 0), (0, 0), (0, held - rows), (0, 0)))
    left = left.reshape(NQ, channels * held, NPB * B)

    share = sector_rows // ops
    psi = lax.dynamic_slice_in_dim(wavefunction, op * share, share, 1).astype(jnp.bfloat16)
    psi = psi.reshape(2, some, share, groups, width).transpose(0, 3, 2, 1, 4)
    psi = psi.reshape(2, groups, share, some * width)
    kept = lax.dynamic_index_in_dim(psi, part, 0, keepdims=False)
    came = lax.ppermute(lax.dynamic_index_in_dim(psi, 1 - part, 0, keepdims=False), "bond", partner)
    piece = jnp.stack([jnp.where(part == 0, kept, came), jnp.where(part == 0, came, kept)])
    gathered = spread(piece, half, ops, 1)
    if width == B:
        psi = gathered.transpose(2, 0, 3, 1, 4, 5).reshape(DP * NB, sector_rows, some * B)
    else:
        psi = gathered.reshape(half, ops, 2, share, some, strip).transpose(2, 0, 5, 1, 3, 4)
        psi = psi.reshape(DP * NB, B, sector_rows, some).transpose(0, 2, 3, 1)
        psi = psi.reshape(DP * NB, sector_rows, some * B)

    def unpack(result):
        result = result.reshape(NB, DP, some, held, B)[:, :, :, :rows]
        return result.reshape(NB, DP, some, NPB, band, B)

    def summed_share(parts, axis):
        size = parts.shape[axis] // ops
        total = lax.dynamic_slice_in_dim(parts, op * size, size, axis)
        for e in range(1, ops):
            to = (op + e) % ops
            sent = lax.dynamic_slice_in_dim(parts, to * size, size, axis)
            total += lax.ppermute(sent, "op", [(o, (o + e) % ops) for o in range(ops)])
        return total

    first = unpack(apply_all(right_order, shift, site, psi, left, right, held, some))
    turned = (DP * NB, some, NPB, band, B)
    if DP % ops == 0:
        first = summed_share(first, 1).transpose(1, 0, 2, 3, 4, 5)
        first = first.reshape((DP * NB // ops,) + turned[1:])
    else:
        first = summed_share(first.transpose(1, 0, 2, 3, 4, 5).reshape(turned), 0)
    blocks = first.shape[0]

    mine = lax.dynamic_index_in_dim(first, part, 2, keepdims=False)
    theirs = lax.dynamic_index_in_dim(first, 1 - part, 2, keepdims=False)
    back = lax.ppermute(theirs.astype(jnp.bfloat16), "bond", partner).astype(jnp.float32)
    both = jnp.stack([jnp.where(part == 0, mine, back), jnp.where(part == 0, back, mine)])
    sigma_one = both.transpose(0, 2, 3, 1, 4).reshape(roots, band, blocks * B)

    again = first.astype(jnp.bfloat16).transpose(0, 2, 3, 1, 4)
    again = again.reshape(blocks, NPB, band, some * B)
    again = spread(again, half, ops, 2)
    again = again.transpose(1, 2, 3, 0, 4, 5).reshape(DP * NB, sector_rows, some * B)
    second = unpack(apply_all(right_order, shift, site, again, left, right, held, some))
    if ops == NPB:
        second = summed_share(second, 3)
    else:
        second = lax.psum(second, "op")
    tiles = second.shape[3]
    second = second.astype(jnp.bfloat16).transpose(2, 3, 4, 1, 0, 5)
    second = second.reshape(some, tiles * band, bonds, strip).transpose(2, 0, 1, 3)
    second = lax.all_to_all(second, "bond", split_axis=0, concat_axis=0, tiled=True)
    second = second.reshape(2, half, some, tiles, band, strip).transpose(0, 2, 3, 1, 4, 5)
    second = second.reshape(roots, tiles * B, strip).astype(jnp.float32)
    if ops != NPB:
        second = lax.dynamic_slice_in_dim(second, op * share, share, 1)
    return (sigma_one, second)


def solution(mesh):
    return jax.shard_map(
        local,
        mesh=mesh,
        in_specs=(
            P(None, None, "bond"),
            P("op", None, None, "bond", None),
            P("op", None, None, "bond", None),
            P("op", None, None),
            P(),
            P(),
            P(),
        ),
        out_specs=(P(None, "bond", "op"), P(None, "op", "bond")),
        check_vma=False,
    )
```

```python
import functools

import jax
import jax.numpy as jnp
from jax import lax
from jax.experimental import pallas as pl
from jax.experimental.pallas import tpu as pltpu
from jax.sharding import PartitionSpec as P

M = 2048
B = 128
NQ = 8
DP = 4
NB = 16
NPB = 2

site_charge_table = (0, 1, 1, 2)
MESH = pl.DeviceIdType.MESH


def site_masks(site_operators, channel_charge):
    site_charge = jnp.array(site_charge_table, dtype=jnp.int32)
    charge_step = site_charge[:, None] - site_charge[None, :]
    allowed = (charge_step[None, :, :] - channel_charge[:, 1][:, None, None]) % NQ == 0
    return jnp.where(allowed, site_operators, jnp.zeros_like(site_operators))


def spread_kernel(half, ops, colours, first, *refs):
    if first:
        x_ref, y_ref, g_ref = refs[:3]
        z_ref = None
        scratch = refs[3:]
    else:
        x_ref, y_ref, g_ref, z_ref = refs[:4]
        scratch = refs[4:]
    own_sem, psend, precv, send_sem, recv_sem, fsend, frecv = scratch
    bond = lax.axis_index("bond")
    o = lax.axis_index("op")
    i = lax.rem(bond, half)
    part = bond // half
    base = bond - i
    partner = i + half * (1 - part)
    bits = half.bit_length() - 1
    streams = 2 if first else 1

    def place(mask):
        at = i
        for t in range(bits):
            if mask >> t & 1:
                at = at + (1 << t) * (1 - 2 * lax.rem(i // (1 << t), 2))
        return at

    def to(bond_index, op_index):
        return {"bond": bond_index, "op": op_index}

    barrier = pltpu.get_barrier_semaphore()
    for t in range(bits):
        pl.semaphore_signal(
            barrier, inc=1, device_id=to(base + place(1 << t), o), device_id_type=MESH
        )
    pl.semaphore_signal(barrier, inc=1, device_id=to(partner, o), device_id_type=MESH)
    for e in range(1, ops):
        pl.semaphore_signal(
            barrier, inc=1, device_id=to(bond, lax.rem(o + e, ops)), device_id_type=MESH
        )
    pl.semaphore_wait(barrier, bits + ops)

    index = (part, 1 - part) if first else (0,)
    exchange = []
    for c in range(colours if first else 1):
        exchange.append(pltpu.make_async_remote_copy(
            src_ref=y_ref.at[c] if first else y_ref,
            dst_ref=g_ref.at[i, o, part, c] if first else z_ref,
            send_sem=psend.at[c], recv_sem=precv.at[c],
            device_id=to(partner, o), device_id_type=MESH,
        ))
        exchange[-1].start()

    copies = {}
    forwards = []
    ready = set()

    def block(s, c, mask):
        if s == 0 and mask == 0:
            return x_ref.at[c]
        return g_ref.at[place(mask), o, index[s], c]

    def ensure(s, c, mask):
        if (s, c, mask) in ready:
            return
        ready.add((s, c, mask))
        if mask:
            copies[s, c, mask].wait_recv()
        elif s == 1:
            exchange[c].wait_recv()
        for e in range(1, ops):
            copy = pltpu.make_async_remote_copy(
                src_ref=block(s, c, mask), dst_ref=g_ref.at[place(mask), o, index[s], c],
                send_sem=fsend.at[s, c, mask, e], recv_sem=frecv.at[s, c, mask, e],
                device_id=to(bond, lax.rem(o + e, ops)), device_id_type=MESH,
            )
            copy.start()
            forwards.append(copy)

    own = pltpu.make_async_copy(x_ref, g_ref.at[i, o, index[0]], own_sem)
    own.start()
    for s in range(streams):
        reached = [[0] for c in range(colours)]
        for step in range(bits):
            for at in range(max(len(r) for r in reached)):
                for c in range(colours):
                    mask = reached[c][at]
                    bit = 1 << (c + step) % bits
                    ensure(s, c, mask)
                    copy = pltpu.make_async_remote_copy(
                        src_ref=block(s, c, mask), dst_ref=g_ref.at[place(mask), o, index[s], c],
                        send_sem=send_sem.at[s, c, mask | bit], recv_sem=recv_sem.at[s, c, mask | bit],
                        device_id=to(base + place(bit), o), device_id_type=MESH,
                    )
                    copy.start()
                    copies[s, c, mask | bit] = copy
            for c in range(colours):
                bit = 1 << (c + step) % bits
                reached[c] = reached[c] + [mask | bit for mask in reached[c]]
    for s in range(streams):
        for mask in range(half):
            for c in range(colours):
                ensure(s, c, mask)
    own.wait()
    for copy in copies.values():
        copy.wait_send()
    for copy in exchange:
        copy.wait_send()
        if not first:
            copy.wait_recv()
    for copy in forwards:
        copy.wait()


def spread(x, y, half, ops, first):
    colours = x.shape[0]
    streams = 2 if first else 1
    shapes = [jax.ShapeDtypeStruct((half, ops, streams) + x.shape, x.dtype)]
    if not first:
        shapes.append(jax.ShapeDtypeStruct(y.shape, y.dtype))
    size = x.size * half * ops * streams * 2
    return pl.pallas_call(
        functools.partial(spread_kernel, half, ops, colours, first),
        out_shape=shapes,
        in_specs=[pl.BlockSpec(memory_space=pltpu.VMEM)] * 2,
        out_specs=[pl.BlockSpec(memory_space=pl.ANY)] * len(shapes),
        scratch_shapes=[
            pltpu.SemaphoreType.DMA,
            pltpu.SemaphoreType.DMA((colours,)),
            pltpu.SemaphoreType.DMA((colours,)),
            pltpu.SemaphoreType.DMA((streams, colours, half)),
            pltpu.SemaphoreType.DMA((streams, colours, half)),
            pltpu.SemaphoreType.DMA((streams, colours, half, ops)),
            pltpu.SemaphoreType.DMA((streams, colours, half, ops)),
        ],
        compiler_params=pltpu.CompilerParams(
            collective_id=1 if first else 2, has_side_effects=True
        ),
        cost_estimate=pl.CostEstimate(flops=0, bytes_accessed=16 * size, transcendentals=0),
        name="spread_first" if first else "spread_second",
    )(x, y)


def apply_kernel(
    channels, rows, roots, site_charges, load,
    order_ref, shift_ref, site_ref, psi_ref, left_ref, right_ref, out_ref, mixed
):
    @pl.loop(0, NQ)
    def _(g):
        for n in range(NPB):
            r = order_ref[g * NPB + n]
            terms = []
            for q in range(DP):
                h = lax.rem(2 * NQ - site_charges[q] - g, NQ)
                terms.append(
                    jnp.dot(left_ref[h], load(psi_ref, q * NB + r), preferred_element_type=jnp.float32)
                )
            for c in range(channels):
                for p in range(DP):
                    total = site_ref[(c * DP + p) * DP] * terms[0][c * rows:(c + 1) * rows]
                    for q in range(1, DP):
                        total += site_ref[(c * DP + p) * DP + q] * terms[q][c * rows:(c + 1) * rows]
                    total = total.astype(jnp.bfloat16)
                    for k in range(roots):
                        at = (p * roots + k) * rows
                        mixed[c, g, at:at + rows, n * B:(n + 1) * B] = total[:, k * B:(k + 1) * B]

    @pl.loop(0, NQ)
    def _(g):
        total = None
        for c in range(channels):
            source = lax.rem(g + shift_ref[c], NQ)
            term = lax.dot_general(
                mixed[c, source], right_ref[c, g], (((1,), (1,)), ((), ())),
                preferred_element_type=jnp.float32,
            )
            total = term if total is None else total + term
        for m in range(NPB):
            out_ref[order_ref[g * NPB + m]] = total[:, m * B:(m + 1) * B]


def apply_all(order, shift, site, psi, left, right, rows, roots, load):
    channels = right.shape[0]
    height = DP * roots * rows
    smem = pl.BlockSpec(memory_space=pltpu.SMEM)
    vmem = pl.BlockSpec(memory_space=pltpu.VMEM)
    return pl.pallas_call(
        functools.partial(apply_kernel, channels, rows, roots, site_charge_table, load),
        out_shape=jax.ShapeDtypeStruct((NB, height, B), jnp.float32),
        in_specs=[smem, smem, smem, vmem, vmem, vmem],
        out_specs=vmem,
        scratch_shapes=[pltpu.VMEM((channels, NQ, height, NPB * B), jnp.bfloat16)],
        compiler_params=pltpu.CompilerParams(vmem_limit_bytes=58 * 1024 * 1024),
        name="apply_all",
    )(order, shift, site, psi, left, right)


def local(
    wavefunction, left_tiles, right_tiles, site_operators, left_charge, right_charge, channel_charge
):
    bonds = lax.axis_size("bond")
    ops = lax.axis_size("op")
    bond = lax.axis_index("bond")
    op = lax.axis_index("op")
    roots, sector_rows, strip = wavefunction.shape
    channels = site_operators.shape[0]
    half = bonds // 2
    part = bond // half
    some = roots // 2
    chunk = left_tiles.shape[3]
    band = 2 * chunk
    rows = NPB * band
    held = -(-rows // 16) * 16
    width = min(strip, B)
    groups = strip // width
    own_charge = lax.dynamic_slice_in_dim(channel_charge, op * channels, channels, 0)
    left_order = jnp.argsort(left_charge, stable=True).astype(jnp.int32)
    right_order = jnp.argsort(right_charge, stable=True).astype(jnp.int32)
    shift = (own_charge[:, 0] + own_charge[:, 1]) % NQ
    site = site_masks(site_operators, own_charge).reshape(-1)

    right = right_tiles[:, right_order].transpose(0, 1, 3, 2, 4).reshape(
        channels, NB, chunk, NPB * B
    )
    right = lax.all_gather(right, "bond", axis=2, tiled=True).reshape(
        channels, NQ, NPB * B, NPB * B
    )

    even = [(b, b // 2 + (b % 2) * half) for b in range(bonds)]
    odd = [(b, b // 2 + (1 - b % 2) * half) for b in range(bonds)]
    one = lax.ppermute(left_tiles, "bond", even)
    two = lax.ppermute(left_tiles, "bond", odd)
    low = jnp.where(part == 0, one, two)
    high = jnp.where(part == 0, two, one)
    left = jnp.concatenate([low, high], axis=3)
    left_slots = ((jnp.arange(NQ)[:, None] + own_charge[None, :, 0]) % NQ)[:, :, None] * NPB + jnp.arange(NPB)
    left = left[jnp.arange(channels)[None, :, None], left_order[left_slots]]
    left = left.transpose(0, 1, 2, 4, 3, 5).reshape(NQ, channels, rows, NPB * B)
    left = jnp.pad(left, ((0, 0), (0, 0), (0, held - rows), (0, 0)))
    left = left.reshape(NQ, channels * held, NPB * B)

    share = sector_rows // ops
    psi = lax.dynamic_slice_in_dim(wavefunction, op * share, share, 1).astype(jnp.bfloat16)
    psi = psi.reshape(2, some, share, groups, width).transpose(0, 1, 3, 2, 4)
    kept = lax.dynamic_index_in_dim(psi, part, 0, keepdims=False)
    other = lax.dynamic_index_in_dim(psi, 1 - part, 0, keepdims=False)
    (psi,) = spread(kept, other, half, ops, True)

    def load_whole(ref, block):
        return ref[block]

    def load_first(ref, block):
        owner = block // groups
        t, j, at = owner // half, lax.rem(owner, half), lax.rem(block, groups)
        return jnp.concatenate(
            [jnp.concatenate([ref[j, o, t, k, at] for o in range(ops)], 0) for k in range(some)], 1
        )

    load = load_first
    if width < B:
        psi = psi.reshape(half, ops, 2, some, share, strip).transpose(2, 0, 5, 1, 4, 3)
        psi = psi.reshape(DP * NB, B, sector_rows, some).transpose(0, 2, 3, 1)
        psi = psi.reshape(DP * NB, sector_rows, some * B)
        load = load_whole
    elif share % 16:
        psi = psi.transpose(2, 0, 4, 1, 5, 3, 6).reshape(DP * NB, sector_rows, some * B)
        load = load_whole

    def unpack(result):
        result = result.reshape(NB, DP, some, held, B)[:, :, :, :rows]
        return result.reshape(NB, DP, some, NPB, band, B)

    def summed_share(parts, axis):
        size = parts.shape[axis] // ops
        total = lax.dynamic_slice_in_dim(parts, op * size, size, axis)
        for e in range(1, ops):
            to = (op + e) % ops
            sent = lax.dynamic_slice_in_dim(parts, to * size, size, axis)
            total += lax.ppermute(sent, "op", [(o, (o + e) % ops) for o in range(ops)])
        return total

    first = unpack(apply_all(right_order, shift, site, psi, left, right, held, some, load))
    turned = (DP * NB, some, NPB, band, B)
    if DP % ops == 0:
        first = summed_share(first, 1).transpose(1, 0, 2, 3, 4, 5)
        first = first.reshape((DP * NB // ops,) + turned[1:])
    else:
        first = summed_share(first.transpose(1, 0, 2, 3, 4, 5).reshape(turned), 0)
    blocks = first.shape[0]

    mine = lax.dynamic_index_in_dim(first, part, 2, keepdims=False)
    theirs = lax.dynamic_index_in_dim(first, 1 - part, 2, keepdims=False)
    again = first.astype(jnp.bfloat16).transpose(1, 0, 2, 3, 4)
    again, back = spread(again, theirs.astype(jnp.bfloat16), half, ops, False)
    back = back.astype(jnp.float32)
    both = jnp.stack([jnp.where(part == 0, mine, back), jnp.where(part == 0, back, mine)])
    sigma_one = both.transpose(0, 2, 3, 1, 4).reshape(roots, band, blocks * B)

    def load_second(ref, block):
        o, at = block // blocks, lax.rem(block, blocks)
        return jnp.concatenate(
            [
                jnp.concatenate([ref[j, o, 0, k, at, m] for m in range(NPB) for j in range(half)], 0)
                for k in range(some)
            ], 1,
        )

    load = load_second
    if band % 16:
        again = again[:, :, 0].transpose(1, 3, 4, 0, 5, 2, 6)
        again = again.reshape(DP * NB, sector_rows, some * B)
        load = load_whole
    second = unpack(apply_all(right_order, shift, site, again, left, right, held, some, load))
    if ops == NPB:
        second = summed_share(second, 3)
    else:
        second = lax.psum(second, "op")
    tiles = second.shape[3]
    second = second.astype(jnp.bfloat16).transpose(2, 3, 4, 1, 0, 5)
    second = second.reshape(some, tiles * band, bonds, strip).transpose(2, 0, 1, 3)
    second = lax.all_to_all(second, "bond", split_axis=0, concat_axis=0, tiled=True)
    second = second.reshape(2, half, some, tiles, band, strip).transpose(0, 2, 3, 1, 4, 5)
    second = second.reshape(roots, tiles * B, strip).astype(jnp.float32)
    if ops != NPB:
        second = lax.dynamic_slice_in_dim(second, op * share, share, 1)
    return (sigma_one, second)


def solution(mesh):
    return jax.shard_map(
        local,
        mesh=mesh,
        in_specs=(
            P(None, None, "bond"),
            P("op", None, None, "bond", None),
            P("op", None, None, "bond", None),
            P("op", None, None),
            P(),
            P(),
            P(),
        ),
        out_specs=(P(None, "bond", "op"), P(None, "op", "bond")),
        check_vma=False,
    )
```
